32 devices in a mesh: ctx: 8 (over z, x), head: 4 (over y, core).
Axes of the slice: x: 2, y: 2, z: 4, core: 2. Of those that a mesh axis runs over, the one named last changes fastest.
Arguments:
- token_keys: bfloat16 [8, 2048, 128], P(None, ('ctx', 'head')), may hold values from -4.5 to 4.5
- token_values: bfloat16 [8, 2048, 128], P(None, ('ctx', 'head')), may hold values from -6 to 6
- queries: bfloat16 [8, 2048, 8, 128], P(None, ('ctx', 'head')), may hold values from -16 to 16
- out_grad: bfloat16 [8, 2048, 8, 128], P(None, ('ctx', 'head')), may hold values from -6 to 6
- slot_ids: int32 [8, 2048], P('head'), may hold values from 0 to 511, as said below
Outputs:
- attended: bfloat16 [8, 2048, 8, 128], P(None, ('ctx', 'head'))
- key_grad: float32 [8, 2048, 128], P(None, ('ctx', 'head'))
- value_grad: float32 [8, 2048, 128], P(None, ('ctx', 'head'))
The draws below stay inside these ranges and needn't reach their ends.
Inputs may be any that keep to these rules, and one draw needn't show every extreme that they name: `slot_ids`: in each head's row slot numbers never fall; each of the 512 slots holds 1 to 16 consecutive tokens; slots k * 64 to (k + 1) * 64 - 1 all begin among tokens k * 256 to (k + 1) * 256 - 1; every such block of tokens holds a slot of exactly 16 tokens.
All inputs are finite; a program needn't handle non-finite values.
Results may differ from the reference program's by a relative error of at most 0.012.
The reference program's roundings to bfloat16 on the way (of `slot_pairs`, `weights_low`, `dscores` and `slot_grads`) count: a program that leaves them out, or rounds other values in their place, can miss the bound.
Values may be sent and summed in bfloat16 or wider, within the bound.
A program may use at most 64 MiB of HBM per device.

```python
import math
import jax
import jax.numpy as jnp
from jax import lax

HEAD_DIM = 128
GROUP = 8
KV_HEADS = 8
RATIO = 4
RUN_MAX = 16
TOK_DEV = 256
CTX = 2048
SLOTS = 512
SLOT_DEV = 64
QUERIES = 2048
STRIDE = 1


def draw_token_keys(key, part):
    base_key = jax.random.fold_in(key, 11)
    shape_all = (KV_HEADS, CTX, HEAD_DIM)
    drawn = jnp.clip(jax.random.normal(base_key, shape_all, jnp.float32), -4.0, 4.0)
    return drawn.astype(jnp.bfloat16)


def draw_queries(key, part):
    base_key = jax.random.fold_in(key, 13)
    shape_all = (KV_HEADS, QUERIES, GROUP, HEAD_DIM)
    drawn = jnp.clip(4.0 * jax.random.normal(base_key, shape_all, jnp.float32), -16.0, 16.0)
    return drawn.astype(jnp.bfloat16)


def draw_slot_ids(key, part):
    blocks = CTX // TOK_DEV
    per_block = SLOT_DEV
    block_index = jnp.arange(blocks, dtype=jnp.int32)
    offsets = jax.random.randint(jax.random.fold_in(key, 21), (KV_HEADS, blocks), 1, 4).astype(jnp.int32)
    offsets = jnp.where(block_index[None, :] == 0, 0, offsets)
    next_off = jnp.concatenate([offsets[:, 1:], jnp.zeros((KV_HEADS, 1), jnp.int32)], axis=1)
    group_at = jax.random.randint(jax.random.fold_in(key, 22), (KV_HEADS, blocks, 1), 0, per_block - 5).astype(jnp.int32)
    amounts = jax.random.randint(jax.random.fold_in(key, 23), (KV_HEADS, blocks, per_block // 2), -3, 4).astype(jnp.int32)
    slot_pos = jnp.arange(per_block, dtype=jnp.int32)[None, None, :]
    in_group = (slot_pos >= group_at) & (slot_pos < group_at + 5)
    group_len = jnp.where(slot_pos == group_at, RUN_MAX, 1)
    rank = jnp.where(slot_pos < group_at, slot_pos, slot_pos - 5)
    pair_index = jnp.clip(rank // 2, 0, per_block // 2 - 1)
    amount = jnp.take_along_axis(amounts, pair_index, axis=2)
    pair_len = RATIO + jnp.where(rank % 2 == 0, amount, -amount)
    last_len = (RATIO + next_off - offsets)[:, :, None]
    lengths = jnp.where(in_group, group_len, jnp.where(slot_pos == per_block - 1, last_len, pair_len)).astype(jnp.int32)
    starts = offsets[:, :, None] + jnp.cumsum(lengths, axis=2) - lengths
    token_pos = jnp.arange(TOK_DEV, dtype=jnp.int32)
    counted = jnp.sum((starts[:, :, None, :] <= token_pos[None, None, :, None]).astype(jnp.int32), axis=3)
    ids = block_index[None, :, None] * per_block + counted - 1
    return ids.reshape(KV_HEADS, CTX).astype(jnp.int32)


def levels(own_key, shape, cuts, smallest, high):
    loudness, own = 1.0, jax.random.fold_in(own_key, 6)
    for axis_at, shards_of in cuts:
        draws = jnp.exp(jax.random.uniform(jax.random.fold_in(own, axis_at), (shards_of,), jnp.float32, smallest / len(cuts), high / len(cuts)))
        loudness = loudness * jnp.repeat(draws, shape[axis_at] // shards_of).reshape([-1 if axis == axis_at else 1 for axis in range(len(shape))])
    return loudness


def gaussian(rng, extent, width, bound, cuts=(), kind=jnp.bfloat16):
    entries = width * jax.random.normal(rng, extent, jnp.float32)
    if cuts:
        entries = entries * levels(rng, extent, cuts, -0.22, 0.18)
    return jnp.clip(entries, -bound, bound).astype(kind)


def setup_inputs(seed: int = 0) -> dict:
    streams_of = jax.random.split(jax.random.key(seed), 6)
    return {
        "token_keys": draw_token_keys(jax.random.fold_in(streams_of[5], 71), 0),
        "token_values": gaussian(streams_of[1], (KV_HEADS, CTX, HEAD_DIM), 1.0, 6.0, ((1, 32),)),
        "queries": draw_queries(jax.random.fold_in(streams_of[5], 71), 0),
        "out_grad": gaussian(streams_of[3], (KV_HEADS, QUERIES, GROUP, HEAD_DIM), 1.0, 6.0, ((1, 32),)),
        "slot_ids": draw_slot_ids(jax.random.fold_in(streams_of[5], 71), 0),
    }


neg_big = -1e+30

def slot_table(id_row):
    slot_edges = jnp.searchsorted(id_row, jnp.arange(SLOTS + 1, dtype=jnp.int32), side='left').astype(jnp.int32)
    return (slot_edges[:-1], slot_edges[1:] - slot_edges[:-1])

def one_head(inputs):
    head_keys, head_values, head_queries, head_grads, id_row = inputs
    slot_start, slot_len = slot_table(id_row)
    lengths = slot_len.astype(jnp.float32)[:, None]
    pair_data = jnp.concatenate([head_keys, head_values], axis=1).astype(jnp.float32)
    slot_sums = jax.ops.segment_sum(pair_data, id_row, num_segments=SLOTS)
    slot_pairs = (slot_sums / lengths).astype(jnp.bfloat16)
    slot_keys = slot_pairs[:, :HEAD_DIM]
    slot_vals = slot_pairs[:, HEAD_DIM:]
    score_scale = 1.0 / math.sqrt(HEAD_DIM)
    total_rows = QUERIES * GROUP
    block_rows = math.gcd(2048, total_rows)
    query_rows = head_queries.reshape(total_rows // block_rows, block_rows, HEAD_DIM)
    grad_rows = head_grads.reshape(total_rows // block_rows, block_rows, HEAD_DIM)
    positions = jnp.arange(QUERIES, dtype=jnp.int32) * STRIDE + STRIDE - 1
    positions = jnp.repeat(positions, GROUP).reshape(total_rows // block_rows, block_rows)

    def scan_step(totals, block_in):
        q_block, g_block, p_block = block_in
        scores = jnp.dot(q_block, slot_keys.T, preferred_element_type=jnp.float32) * score_scale
        visible = slot_start[None, :] <= p_block[:, None]
        row_top = lax.optimization_barrier(jnp.max(jnp.where(visible, scores, neg_big), axis=1, keepdims=True))
        raw_weights = jnp.where(visible, jnp.exp(scores - row_top), 0.0)
        weights = raw_weights / lax.optimization_barrier(jnp.sum(raw_weights, axis=1, keepdims=True))
        weights_low = weights.astype(jnp.bfloat16)
        attended = jnp.dot(weights_low, slot_vals, preferred_element_type=jnp.float32).astype(jnp.bfloat16)
        row_dot = lax.optimization_barrier(jnp.sum(g_block.astype(jnp.float32) * attended.astype(jnp.float32), axis=1, keepdims=True))
        weight_grads = jnp.dot(g_block, slot_vals.T, preferred_element_type=jnp.float32)
        dscores = (weights * (weight_grads - row_dot)).astype(jnp.bfloat16)
        value_grads = jnp.dot(weights_low.T, g_block, preferred_element_type=jnp.float32)
        key_grads = jnp.dot(dscores.T, q_block, preferred_element_type=jnp.float32) * score_scale
        return ((totals[0] + key_grads, totals[1] + value_grads), attended)
    zeros_init = jnp.zeros((SLOTS, HEAD_DIM), jnp.float32)
    (key_grads, value_grads), attended = lax.scan(scan_step, (zeros_init, zeros_init), (query_rows, grad_rows, positions))
    slot_grads = jnp.concatenate([key_grads, value_grads], axis=1).astype(jnp.bfloat16)
    token_grads = slot_grads[id_row].astype(jnp.float32) / lengths[id_row]
    return (attended.reshape(QUERIES, GROUP, HEAD_DIM), token_grads[:, :HEAD_DIM], token_grads[:, HEAD_DIM:])

def reference(token_keys, token_values, queries, out_grad, slot_ids):
    attended, key_grad, value_grad = lax.map(one_head, (token_keys, token_values, queries, out_grad, slot_ids))
    return (attended, key_grad, value_grad)
```

```python
import functools
import math

import jax
import jax.numpy as jnp
from jax import lax
from jax.experimental import pallas as pl
from jax.experimental.pallas import tpu as pltpu
from jax.sharding import PartitionSpec as P

RATIO = 4
EDGE = 16
LANES = 128
MESH = pl.DeviceIdType.MESH
neg_big = -1e30


def dot_nt(a, b):
    return lax.dot_general(a, b, (((1,), (1,)), ((), ())), preferred_element_type=jnp.float32)


def dot_tn(a, b):
    return lax.dot_general(a, b, (((0,), (0,)), ((), ())), preferred_element_type=jnp.float32)


def dot_nn(a, b):
    return lax.dot_general(a, b, (((1,), (0,)), ((), ())), preferred_element_type=jnp.float32)


def kernel(
    dims,
    q_ref, g_ref, k_ref, v_ref, id_ref, thr_ref,
    out_ref, kg_ref, vg_ref,
    qb, gb, tk, tv, ek, ev, thrb, pairs, att, part, rs, acc, tg, tgx, rt, rx,
    q_s, q_r, g_s, g_r, loc, tok_s, tok_r, ext_s, ext_r, thr_s, thr_r,
    ag_s, ag_r, fw_s, fw_r, at_s, at_r, rs_s, rs_r, tg_s, tg_r, tx_s, tx_r,
):
    nc, nh, hpd, T, R, S, D = dims
    ny = nh // 2
    TB = T * nh
    NS = nc * S
    scale = 1.0 / math.sqrt(D)
    ctx = lax.axis_index("ctx")
    j = lax.axis_index("head")
    y, c = j // 2, lax.rem(j, 2)
    peer = y * 2 + 1 - c

    def remote(src, dst, ssem, rsem, to_ctx, to_head):
        return pltpu.make_async_remote_copy(
            src_ref=src, dst_ref=dst, send_sem=ssem, recv_sem=rsem,
            device_id=(to_ctx, to_head), device_id_type=MESH,
        )

    def heads(ref, owner):
        return ref.at[pl.ds(owner * hpd, hpd)]

    ek[...] = jnp.zeros_like(ek)
    ev[...] = jnp.zeros_like(ev)
    rx[...] = jnp.zeros_like(rx)

    @pl.loop(0, nc)
    def _(b):
        @pl.when(b > ctx)
        def _():
            for yy in range(ny):
                for h in range(hpd):
                    pairs[yy, h, b] = jnp.zeros((S, 2 * D), jnp.bfloat16)

    barrier = pltpu.get_barrier_semaphore()
    me = ctx * nh + j

    @pl.loop(1, nc * nh)
    def _(i):
        other = lax.rem(me + i, nc * nh)
        pl.semaphore_signal(
            barrier, inc=1, device_id=(other // nh, lax.rem(other, nh)), device_id_type=MESH
        )

    pl.semaphore_wait(barrier, nc * nh - 1)

    def tok_copy(to, frm, kv):
        src, dst = ((k_ref, tk), (v_ref, tv))[kv]
        return remote(heads(src, to), dst.at[:, frm], tok_s.at[to, kv], tok_r.at[frm, kv], ctx, to)

    def ext_copy(to_ctx, to, kv):
        src, dst = ((k_ref, ek), (v_ref, ev))[kv]
        return remote(
            src.at[pl.ds(to * hpd, hpd), pl.ds(0, EDGE)], dst.at[:, pl.ds(0, EDGE)],
            ext_s.at[to, kv], ext_r.at[kv], to_ctx, to,
        )

    def thr_copy(to_y, frm_y):
        return remote(thr_ref.at[to_y], thrb.at[frm_y], thr_s.at[to_y], thr_r.at[frm_y], ctx, to_y * 2 + c)

    def swap_copy(yy, kv, core):
        src, dst, ss, sr = ((q_ref, qb, q_s, q_r), (g_ref, gb, g_s, g_r))[kv]
        return remote(
            heads(src, yy * 2 + 1 - c), dst.at[yy, :, core], ss.at[yy], sr.at[yy], ctx, peer
        )

    def ag_copy(to_ctx, frm):
        blk = pairs.at[y, :, frm]
        return remote(blk, blk, ag_s.at[to_ctx], ag_r.at[frm], to_ctx, j)

    def fw_copy(to_y, frm_y, b):
        blk = pairs.at[frm_y, :, b]
        return remote(blk, blk, fw_s.at[to_y, b], fw_r.at[frm_y, b], ctx, to_y * 2 + c)

    def att_copy(yy):
        return remote(att.at[yy, :, 1 - c], heads(out_ref, yy * 2 + c), at_s.at[yy], at_r.at[yy], ctx, peer)

    def att_in(yy):
        return remote(att.at[yy, :, 1 - c], heads(out_ref, yy * 2 + 1 - c), at_s.at[yy], at_r.at[yy], ctx, peer)

    def rs_copy(yy, b, frm_ctx, frm_y):
        return remote(
            part.at[yy, :, b], rs.at[frm_ctx, frm_y], rs_s.at[yy, b], rs_r.at[frm_ctx, frm_y], b, yy * 2 + c
        )

    def tg_copy(to, frm):
        return remote(tg.at[to], rt.at[frm], tg_s.at[to], tg_r.at[frm], ctx, to)

    def tx_copy(to_ctx, frm):
        return remote(tgx, rx.at[frm], tx_s, tx_r.at[frm], to_ctx, 0)

    for d in range(1, nh):
        to = lax.rem(j + d, nh)
        tok_copy(to, j, 0).start()
        tok_copy(to, j, 1).start()

    @pl.when((j == 0) & (ctx > 0))
    def _():
        for to in range(nh):
            ext_copy(ctx - 1, to, 0).start()
            ext_copy(ctx - 1, to, 1).start()

    own_tok = [
        pltpu.make_async_copy(heads(k_ref, j), tk.at[:, j], loc.at[0]),
        pltpu.make_async_copy(heads(v_ref, j), tv.at[:, j], loc.at[1]),
    ]
    own_thr = pltpu.make_async_copy(thr_ref.at[y], thrb.at[y], loc.at[2])
    for cp in own_tok:
        cp.start()
    own_thr.start()
    for d in range(1, ny):
        thr_copy(lax.rem(y + d, ny), y).start()
    own_rows = []
    for d in range(ny):
        yy = lax.rem(y + d, ny)
        swap_copy(yy, 0, c).start()
        swap_copy(yy, 1, c).start()
        own_rows.append(
            pltpu.make_async_copy(heads(q_ref, yy * 2 + c), qb.at[yy, :, c], loc.at[3 + 2 * d])
        )
        own_rows.append(
            pltpu.make_async_copy(heads(g_ref, yy * 2 + c), gb.at[yy, :, c], loc.at[4 + 2 * d])
        )
    for cp in own_rows:
        cp.start()

    for d in range(1, nh):
        frm = lax.rem(j + d, nh)
        tok_copy(j, frm, 0).wait_recv()
        tok_copy(j, frm, 1).wait_recv()

    @pl.when(ctx < nc - 1)
    def _():
        ext_copy(ctx, j, 0).wait_recv()
        ext_copy(ctx, j, 1).wait_recv()

    for cp in own_tok:
        cp.wait()

    def hot(h):
        rel = id_ref[h]
        main = lax.broadcasted_iota(jnp.int32, (S, TB), 0) == rel[:, :TB]
        edge = lax.broadcasted_iota(jnp.int32, (S, LANES), 0) == rel[:, TB:]
        main, edge = main.astype(jnp.float32), edge.astype(jnp.float32)
        count = jnp.sum(main, axis=1, keepdims=True) + jnp.sum(edge, axis=1, keepdims=True)
        return main.astype(jnp.bfloat16), edge.astype(jnp.bfloat16), count

    for h in range(hpd):
        main, edge, count = hot(h)
        keys = dot_nn(main, tk[h].reshape(TB, D)) + dot_nn(edge, ek[h])
        vals = dot_nn(main, tv[h].reshape(TB, D)) + dot_nn(edge, ev[h])
        pairs[y, h, ctx, :, :D] = (keys / count).astype(jnp.bfloat16)
        pairs[y, h, ctx, :, D:] = (vals / count).astype(jnp.bfloat16)

    @pl.loop(0, nc)
    def _(i):
        to = nc - 1 - i

        @pl.when(to > ctx)
        def _():
            ag_copy(to, ctx).start()

    for d in range(1, ny):
        fw_copy(lax.rem(y + d, ny), y, ctx).start()

    for cp in own_rows:
        cp.wait()
    own_thr.wait()
    for d in range(ny):
        yy = lax.rem(y + d, ny)
        swap_copy(yy, 0, 1 - c).wait_recv()
        swap_copy(yy, 1, 1 - c).wait_recv()

    @pl.loop(0, nc)
    def _(i):
        b = nc - 1 - i

        @pl.when(b < ctx)
        def _():
            ag_copy(ctx, b).wait_recv()
            for d in range(1, ny):
                fw_copy(lax.rem(y + d, ny), y, b).start()

    @pl.loop(0, ny)
    def _(k):
        yy = lax.rem(y + k, ny)

        @pl.when(k > 0)
        def _():
            thr_copy(y, yy).wait_recv()

            @pl.loop(0, nc)
            def _(b):
                @pl.when(b <= ctx)
                def _():
                    fw_copy(y, yy, b).wait_recv()

        @pl.loop(0, hpd)
        def _(h):
            both = pairs[yy, h].reshape(NS, 2 * D)
            keys, vals = both[:, :D], both[:, D:]
            slot = lax.broadcasted_iota(jnp.int32, (NS, R), 0)
            key_sum = val_sum = None
            for core in range(2):
                rows, grads = qb[yy, h, core], gb[yy, h, core]
                scores = jnp.where(slot <= thrb[yy, h, core], dot_nt(keys, rows), neg_big)
                top = jnp.max(scores, axis=0, keepdims=True)
                raw = jnp.exp2((scores - top) * (scale * math.log2(math.e)))
                weights = raw * (1.0 / jnp.sum(raw, axis=0, keepdims=True))
                low = weights.astype(jnp.bfloat16)
                seen = dot_tn(vals, low).astype(jnp.bfloat16).astype(jnp.float32)
                grads_t = grads.astype(jnp.float32).T
                row_dot = jnp.sum(grads_t * seen, axis=0, keepdims=True)
                att[yy, h, core] = seen.T.astype(jnp.bfloat16)
                slope = (weights * (dot_nt(vals, grads) - row_dot)).astype(jnp.bfloat16)
                val_grad = dot_nn(low, grads)
                key_grad = dot_nn(slope, rows)
                key_sum = key_grad if key_sum is None else key_sum + key_grad
                val_sum = val_grad if val_sum is None else val_sum + val_grad
            part[yy, h, :, :, :D] = (key_sum * scale).astype(jnp.bfloat16).reshape(nc, S, D)
            part[yy, h, :, :, D:] = val_sum.astype(jnp.bfloat16).reshape(nc, S, D)

        @pl.loop(0, nc)
        def _(b):
            @pl.when((b < ctx) | ((b == ctx) & (k > 0)))
            def _():
                rs_copy(yy, b, ctx, y).start()

        att_copy(yy).start()
        pltpu.make_async_copy(att.at[yy, :, c], heads(out_ref, yy * 2 + c), loc.at[3 + yy]).start()

    for h in range(hpd):
        acc[h] = part[y, h, ctx].astype(jnp.float32)

    @pl.loop(0, nc)
    def _(b):
        for yy in range(ny):
            @pl.when((b > ctx) | ((b == ctx) & (y != yy)))
            def _():
                rs_copy(y, ctx, b, yy).wait_recv()
                for h in range(hpd):
                    acc[h] += rs[b, yy, h].astype(jnp.float32)

    for h in range(hpd):
        main, edge, count = hot(h)
        unit = (acc[h].astype(jnp.bfloat16).astype(jnp.float32) / count).astype(jnp.bfloat16)
        spread = dot_tn(main, unit).astype(jnp.bfloat16)
        for to in range(nh):
            tg[to, h] = spread[to * T:(to + 1) * T]
        tgx[h] = dot_tn(edge, unit)[:EDGE].astype(jnp.bfloat16)

    for d in range(1, nh):
        tg_copy(lax.rem(j + d, nh), j).start()

    @pl.when((ctx < nc - 1))
    def _():
        @pl.when((ctx >= 0))
        def _():
            tx_copy(ctx + 1, j).start()

    own_tg = pltpu.make_async_copy(tg.at[j], rt.at[j], loc.at[0])
    own_tg.start()

    for d in range(1, nh):
        to = lax.rem(j + d, nh)
        tok_copy(to, j, 0).wait_send()
        tok_copy(to, j, 1).wait_send()

    @pl.when((j == 0) & (ctx > 0))
    def _():
        for to in range(nh):
            ext_copy(ctx - 1, to, 0).wait_send()
            ext_copy(ctx - 1, to, 1).wait_send()

    for d in range(1, ny):
        thr_copy(lax.rem(y + d, ny), y).wait_send()
    for yy in range(ny):
        swap_copy(yy, 0, c).wait_send()
        swap_copy(yy, 1, c).wait_send()
        att_copy(yy).wait_send()
        att_in(yy).wait_recv()
        pltpu.make_async_copy(att.at[yy, :, c], heads(out_ref, yy * 2 + c), loc.at[3 + yy]).wait()

    @pl.loop(0, nc)
    def _(b):
        @pl.when(b > ctx)
        def _():
            ag_copy(b, ctx).wait_send()

        @pl.when(b <= ctx)
        def _():
            for d in range(1, ny):
                yy = lax.rem(y + d, ny)
                fw_copy(yy, y, b).wait_send()
                rs_copy(yy, b, ctx, y).wait_send()

        @pl.when(b < ctx)
        def _():
            rs_copy(y, b, ctx, y).wait_send()

    own_tg.wait()
    for d in range(1, nh):
        tg_copy(j, lax.rem(j + d, nh)).wait_recv()
    for owner in range(nh):
        for h in range(hpd):
            rows = rt[owner, h].astype(jnp.float32)
            kg_ref[owner * hpd + h] = rows[:, :D]
            vg_ref[owner * hpd + h] = rows[:, D:]

    @pl.when((j == 0) & (ctx > 0))
    def _():
        for owner in range(nh):
            tx_copy(ctx, owner).wait_recv()
            for h in range(hpd):
                rows = rx[owner, h].astype(jnp.float32)
                kg_ref[owner * hpd + h, :EDGE] += rows[:, :D]
                vg_ref[owner * hpd + h, :EDGE] += rows[:, D:]

    for d in range(1, nh):
        tg_copy(lax.rem(j + d, nh), j).wait_send()

    @pl.when((ctx < nc - 1))
    def _():
        tx_copy(ctx + 1, j).wait_send()


def per_device(nc, nh, token_keys, token_values, queries, out_grad, slot_ids):
    heads_all, T, D = token_keys.shape
    group = queries.shape[2]
    hpd, context = slot_ids.shape
    R = queries.shape[1] * group
    stride = T // queries.shape[1]
    TB = T * nh
    S = TB // RATIO
    ny = nh // 2
    ctx = lax.axis_index("ctx")
    padded = jnp.pad(slot_ids, ((0, 0), (0, LANES)), constant_values=context)
    window = lax.dynamic_slice_in_dim(padded, ctx * TB, TB + LANES, 1)
    relative = (window - ctx * S).reshape(hpd, 1, TB + LANES)
    seen_at = window[:, stride - 1:TB:stride]
    limit = jnp.repeat(seen_at.reshape(hpd, ny, 2, 1, R // group), group, axis=4)
    limit = limit.transpose(1, 0, 2, 3, 4)
    bf, f32 = jnp.bfloat16, jnp.float32
    dma = pltpu.SemaphoreType.DMA
    anywhere = pl.BlockSpec(memory_space=pl.ANY)
    vmem = pl.BlockSpec(memory_space=pltpu.VMEM)
    attended, key_grad, value_grad = pl.pallas_call(
        functools.partial(kernel, (nc, nh, hpd, T, R, S, D)),
        out_shape=(
            jax.ShapeDtypeStruct((heads_all, R, D), bf),
            jax.ShapeDtypeStruct((heads_all, T, D), f32),
            jax.ShapeDtypeStruct((heads_all, T, D), f32),
        ),
        in_specs=[anywhere] * 4 + [vmem, vmem],
        out_specs=(anywhere, vmem, vmem),
        scratch_shapes=[
            pltpu.VMEM((ny, hpd, 2, R, D), bf),
            pltpu.VMEM((ny, hpd, 2, R, D), bf),
            pltpu.VMEM((hpd, nh, T, D), bf),
            pltpu.VMEM((hpd, nh, T, D), bf),
            pltpu.VMEM((hpd, LANES, D), bf),
            pltpu.VMEM((hpd, LANES, D), bf),
            pltpu.VMEM((ny, hpd, 2, 1, R), jnp.int32),
            pltpu.VMEM((ny, hpd, nc, S, 2 * D), bf),
            pltpu.VMEM((ny, hpd, 2, R, D), bf),
            pltpu.VMEM((ny, hpd, nc, S, 2 * D), bf),
            pltpu.VMEM((nc, ny, hpd, S, 2 * D), bf),
            pltpu.VMEM((hpd, S, 2 * D), f32),
            pltpu.VMEM((nh, hpd, T, 2 * D), bf),
            pltpu.VMEM((hpd, EDGE, 2 * D), bf),
            pltpu.VMEM((nh, hpd, T, 2 * D), bf),
            pltpu.VMEM((nh, hpd, EDGE, 2 * D), bf),
            dma((ny,)), dma((ny,)), dma((ny,)), dma((ny,)), dma((3 + 2 * ny,)),
            dma((nh, 2)), dma((nh, 2)), dma((nh, 2)), dma((2,)), dma((ny,)), dma((ny,)),
            dma((nc,)), dma((nc,)), dma((ny, nc)), dma((ny, nc)), dma((ny,)), dma((ny,)),
            dma((ny, nc)), dma((nc, ny)), dma((nh,)), dma((nh,)), dma(()), dma((nh,)),
        ],
        compiler_params=pltpu.CompilerParams(
            collective_id=0, has_side_effects=True, vmem_limit_bytes=56 << 20
        ),
    )(
        queries.reshape(heads_all, R, D), out_grad.reshape(heads_all, R, D),
        token_keys, token_values, relative, limit,
    )
    return attended.reshape(queries.shape), key_grad, value_grad


def solution(mesh):
    nc, nh = mesh.shape["ctx"], mesh.shape["head"]
    rows = P(None, ("ctx", "head"), None)
    grouped = P(None, ("ctx", "head"), None, None)
    return jax.shard_map(
        functools.partial(per_device, nc, nh),
        mesh=mesh,
        in_specs=(rows, rows, grouped, grouped, P("head", None)),
        out_specs=(grouped, rows, rows),
        check_vma=False,
    )
```

```python
import functools
import math

import jax
import jax.numpy as jnp
from jax import lax
from jax.experimental import pallas as pl
from jax.experimental.pallas import tpu as pltpu
from jax.sharding import PartitionSpec as P

RATIO = 4
EDGE = 16
LANES = 128
MESH = pl.DeviceIdType.MESH
neg_big = -1e30


def dot_nt(a, b):
    return lax.dot_general(a, b, (((1,), (1,)), ((), ())), preferred_element_type=jnp.float32)


def dot_tn(a, b):
    return lax.dot_general(a, b, (((0,), (0,)), ((), ())), preferred_element_type=jnp.float32)


def dot_nn(a, b):
    return lax.dot_general(a, b, (((1,), (0,)), ((), ())), preferred_element_type=jnp.float32)


def kernel(
    dims,
    q_ref, g_ref, k_ref, v_ref, id_ref, thr_ref,
    out_ref, kg_ref, vg_ref,
    qb, gb, tk, tv, ek, ev, thrb, pk, pv, att, part, ys, rs, acc, tg, tgx, rt, rx,
    q_s, q_r, g_s, g_r, loc, tok_s, tok_r, ext_s, ext_r, thr_s, thr_r,
    ag_s, ag_r, kx_s, kx_r, ky_s, ky_r, vy_s, vy_r, vx_s, vx_r, at_s, at_r,
    ys_s, ys_r, rs_s, rs_r, tg_s, tg_r, tx_s, tx_r,
):
    nc, nx, nh, hpd, T, R, S, D = dims
    ny, nz = nh // 2, nc // nx
    TB = T * nh
    NS = nc * S
    scale = 1.0 / math.sqrt(D)
    ctx = lax.axis_index("ctx")
    j = lax.axis_index("head")
    y, c = j // 2, lax.rem(j, 2)
    peer = y * 2 + 1 - c
    z, x = ctx // nx, lax.rem(ctx, nx)

    def remote(src, dst, ssem, rsem, to_ctx, to_head):
        return pltpu.make_async_remote_copy(
            src_ref=src, dst_ref=dst, send_sem=ssem, recv_sem=rsem,
            device_id=(to_ctx, to_head), device_id_type=MESH,
        )

    def heads(ref, owner):
        return ref.at[pl.ds(owner * hpd, hpd)]

    ek[...] = jnp.zeros_like(ek)
    ev[...] = jnp.zeros_like(ev)
    rx[...] = jnp.zeros_like(rx)

    @pl.loop(0, nc)
    def _(b):
        @pl.when(b > ctx)
        def _():
            for yy in range(ny):
                for h in range(hpd):
                    pk[yy, h, b] = jnp.zeros((S, D), jnp.bfloat16)
                    pv[yy, h, b] = jnp.zeros((S, D), jnp.bfloat16)

    barrier = pltpu.get_barrier_semaphore()
    me = ctx * nh + j

    @pl.loop(1, nc * nh)
    def _(i):
        other = lax.rem(me + i, nc * nh)
        pl.semaphore_signal(
            barrier, inc=1, device_id=(other // nh, lax.rem(other, nh)), device_id_type=MESH
        )

    pl.semaphore_wait(barrier, nc * nh - 1)

    def tok_copy(to, frm, kv):
        src, dst = ((k_ref, tk), (v_ref, tv))[kv]
        return remote(heads(src, to), dst.at[:, frm], tok_s.at[to, kv], tok_r.at[frm, kv], ctx, to)

    def ext_copy(to_ctx, to, kv):
        src, dst = ((k_ref, ek), (v_ref, ev))[kv]
        return remote(
            src.at[pl.ds(to * hpd, hpd), pl.ds(0, EDGE)], dst.at[:, pl.ds(0, EDGE)],
            ext_s.at[to, kv], ext_r.at[kv], to_ctx, to,
        )

    def thr_copy(to_y, frm_y):
        return remote(thr_ref.at[to_y], thrb.at[frm_y], thr_s.at[to_y], thr_r.at[frm_y], ctx, to_y * 2 + c)

    def swap_copy(yy, kv, core):
        src, dst, ss, sr = ((q_ref, qb, q_s, q_r), (g_ref, gb, g_s, g_r))[kv]
        return remote(
            heads(src, yy * 2 + 1 - c), dst.at[yy, :, core], ss.at[yy], sr.at[yy], ctx, peer
        )

    def ag_copy(to_z, frm_z, kv):
        blk = (pk, pv)[kv].at[y, :, frm_z * nx + x]
        return remote(blk, blk, ag_s.at[to_z, kv], ag_r.at[frm_z, kv], to_z * nx + x, j)

    def kx_copy(to_x, frm_x, zs):
        blk = pk.at[y, :, zs * nx + frm_x]
        return remote(blk, blk, kx_s.at[to_x, zs], kx_r.at[frm_x, zs], z * nx + to_x, j)

    def ky_copy(to_y, frm_y, b):
        blk = pk.at[frm_y, :, b]
        return remote(blk, blk, ky_s.at[to_y, b], ky_r.at[frm_y, b], ctx, to_y * 2 + c)

    def vy_copy(to_y, frm_y, zs):
        blk = pv.at[frm_y, :, zs * nx + x]
        return remote(blk, blk, vy_s.at[to_y, zs], vy_r.at[frm_y, zs], ctx, to_y * 2 + c)

    def vx_copy(to_x, frm_x, yy, zs):
        blk = pv.at[yy, :, zs * nx + frm_x]
        return remote(blk, blk, vx_s.at[to_x, yy, zs], vx_r.at[frm_x, yy, zs], z * nx + to_x, j)

    def x_sees(to_x, zs):
        return (zs < z) | ((zs == z) & (to_x > x))

    def x_gives(frm_x, zs):
        return (zs < z) | ((zs == z) & (frm_x < x))

    def att_copy(yy):
        return remote(att.at[yy, :, 1 - c], heads(out_ref, yy * 2 + c), at_s.at[yy], at_r.at[yy], ctx, peer)

    def att_in(yy):
        return remote(att.at[yy, :, 1 - c], heads(out_ref, yy * 2 + 1 - c), at_s.at[yy], at_r.at[yy], ctx, peer)

    def ys_copy(to_y, frm_y, h, b):
        return remote(
            part.at[to_y, h, b], ys.at[frm_y, h, b], ys_s.at[to_y, h, b], ys_r.at[frm_y, h, b], ctx, to_y * 2 + c
        )

    def rs_copy(b, frm_ctx):
        return remote(part.at[y, :, b], rs.at[frm_ctx], rs_s.at[b], rs_r.at[frm_ctx], b, j)

    def tg_copy(to, frm):
        return remote(tg.at[to], rt.at[frm], tg_s.at[to], tg_r.at[frm], ctx, to)

    def tx_copy(to_ctx, frm):
        return remote(tgx, rx.at[frm], tx_s, tx_r.at[frm], to_ctx, 0)

    for d in range(1, nh):
        to = lax.rem(j + d, nh)
        tok_copy(to, j, 0).start()
        tok_copy(to, j, 1).start()

    @pl.when((j == 0) & (ctx > 0))
    def _():
        for to in range(nh):
            ext_copy(ctx - 1, to, 0).start()
            ext_copy(ctx - 1, to, 1).start()

    own_tok = [
        pltpu.make_async_copy(heads(k_ref, j), tk.at[:, j], loc.at[0]),
        pltpu.make_async_copy(heads(v_ref, j), tv.at[:, j], loc.at[1]),
    ]
    own_thr = pltpu.make_async_copy(thr_ref.at[y], thrb.at[y], loc.at[2])
    for cp in own_tok:
        cp.start()
    own_thr.start()
    for d in range(1, ny):
        thr_copy(lax.rem(y + d, ny), y).start()
    own_rows = []
    for d in range(ny):
        yy = lax.rem(y + d, ny)
        swap_copy(yy, 0, c).start()
        swap_copy(yy, 1, c).start()
        own_rows.append(
            pltpu.make_async_copy(heads(q_ref, yy * 2 + c), qb.at[yy, :, c], loc.at[3 + 2 * d])
        )
        own_rows.append(
            pltpu.make_async_copy(heads(g_ref, yy * 2 + c), gb.at[yy, :, c], loc.at[4 + 2 * d])
        )
    for cp in own_rows:
        cp.start()

    for d in range(1, nh):
        frm = lax.rem(j + d, nh)
        tok_copy(j, frm, 0).wait_recv()
        tok_copy(j, frm, 1).wait_recv()

    @pl.when(ctx < nc - 1)
    def _():
        ext_copy(ctx, j, 0).wait_recv()
        ext_copy(ctx, j, 1).wait_recv()

    for cp in own_tok:
        cp.wait()

    def hot(h):
        rel = id_ref[h]
        main = lax.broadcasted_iota(jnp.int32, (S, TB), 0) == rel[:, :TB]
        edge = lax.broadcasted_iota(jnp.int32, (S, LANES), 0) == rel[:, TB:]
        main, edge = main.astype(jnp.float32), edge.astype(jnp.float32)
        count = jnp.sum(main, axis=1, keepdims=True) + jnp.sum(edge, axis=1, keepdims=True)
        return main.astype(jnp.bfloat16), edge.astype(jnp.bfloat16), count

    for h in range(hpd):
        main, edge, count = hot(h)
        keys = dot_nn(main, tk[h].reshape(TB, D)) + dot_nn(edge, ek[h])
        vals = dot_nn(main, tv[h].reshape(TB, D)) + dot_nn(edge, ev[h])
        pk[y, h, ctx] = (keys / count).astype(jnp.bfloat16)
        pv[y, h, ctx] = (vals / count).astype(jnp.bfloat16)

    def spread_block(zs):
        for d in range(1, nx):
            to = lax.rem(x + d, nx)

            @pl.when(x_sees(to, zs))
            def _():
                kx_copy(to, x, zs).start()

        for d in range(1, ny):
            to = lax.rem(y + d, ny)
            vy_copy(to, y, zs).start()
            ky_copy(to, y, zs * nx + x).start()

        for d in range(1, nx):
            to = lax.rem(x + d, nx)

            @pl.when(x_sees(to, zs))
            def _():
                vx_copy(to, x, y, zs).start()

    @pl.loop(0, nz)
    def _(i):
        to = nz - 1 - i

        @pl.when(to > z)
        def _():
            ag_copy(to, z, 0).start()
            ag_copy(to, z, 1).start()

    spread_block(z)

    for cp in own_rows:
        cp.wait()
    own_thr.wait()
    for d in range(ny):
        yy = lax.rem(y + d, ny)
        swap_copy(yy, 0, 1 - c).wait_recv()
        swap_copy(yy, 1, 1 - c).wait_recv()

    @pl.loop(0, nz)
    def _(i):
        zs = nz - 1 - i

        @pl.when(zs < z)
        def _():
            ag_copy(z, zs, 0).wait_recv()
            ag_copy(z, zs, 1).wait_recv()
            spread_block(zs)

    @pl.loop(0, nz)
    def _(i):
        zs = nz - 1 - i

        @pl.when(zs <= z)
        def _():
            for d in range(1, nx):
                frm = lax.rem(x + d, nx)

                @pl.when(x_gives(frm, zs))
                def _():
                    kx_copy(x, frm, zs).wait_recv()
                    for e in range(1, ny):
                        ky_copy(lax.rem(y + e, ny), y, zs * nx + frm).start()

            for e in range(1, ny):
                frm_y = lax.rem(y + e, ny)
                vy_copy(y, frm_y, zs).wait_recv()
                for d in range(1, nx):
                    to = lax.rem(x + d, nx)

                    @pl.when(x_sees(to, zs))
                    def _():
                        vx_copy(to, x, frm_y, zs).start()

    def wait_vals(yy):
        @pl.loop(0, nz)
        def _(zs):
            for d in range(1, nx):
                frm = lax.rem(x + d, nx)

                @pl.when(x_gives(frm, zs))
                def _():
                    vx_copy(x, frm, yy, zs).wait_recv()

    @pl.loop(0, ny)
    def _(k):
        yy = lax.rem(y + k, ny)

        @pl.when(k > 0)
        def _():
            thr_copy(y, yy).wait_recv()

            @pl.loop(0, nc)
            def _(b):
                @pl.when(b <= ctx)
                def _():
                    ky_copy(y, yy, b).wait_recv()

        wait_vals(yy)

        @pl.loop(0, hpd)
        def _(h):
            keys, vals = pk[yy, h].reshape(NS, D), pv[yy, h].reshape(NS, D)
            slot = lax.broadcasted_iota(jnp.int32, (NS, R), 0)
            key_sum = val_sum = None
            for core in range(2):
                rows, grads = qb[yy, h, core], gb[yy, h, core]
                scores = jnp.where(slot <= thrb[yy, h, core], dot_nt(keys, rows), neg_big)
                top = jnp.max(scores, axis=0, keepdims=True)
                raw = jnp.exp2((scores - top) * (scale * math.log2(math.e)))
                weights = raw * (1.0 / jnp.sum(raw, axis=0, keepdims=True))
                low = weights.astype(jnp.bfloat16)
                seen = dot_tn(vals, low).astype(jnp.bfloat16).astype(jnp.float32)
                grads_t = grads.astype(jnp.float32).T
                row_dot = jnp.sum(grads_t * seen, axis=0, keepdims=True)
                att[yy, h, core] = seen.T.astype(jnp.bfloat16)
                slope = (weights * (dot_nt(vals, grads) - row_dot)).astype(jnp.bfloat16)
                val_grad = dot_nn(low, grads)
                key_grad = dot_nn(slope, rows)
                key_sum = key_grad if key_sum is None else key_sum + key_grad
                val_sum = val_grad if val_sum is None else val_sum + val_grad
            part[yy, h, :, :, :D] = (key_sum * scale).astype(jnp.bfloat16).reshape(nc, S, D)
            part[yy, h, :, :, D:] = val_sum.astype(jnp.bfloat16).reshape(nc, S, D)

            @pl.when(k > 0)
            def _():
                @pl.loop(0, nc)
                def _(b):
                    @pl.when(b <= ctx)
                    def _():
                        ys_copy(yy, y, h, b).start()

        att_copy(yy).start()
        pltpu.make_async_copy(att.at[yy, :, c], heads(out_ref, yy * 2 + c), loc.at[3 + yy]).start()

    @pl.loop(0, nc)
    def _(b):
        @pl.when(b <= ctx)
        def _():
            for h in range(hpd):
                total = part[y, h, b].astype(jnp.float32)
                for d in range(1, ny):
                    frm_y = lax.rem(y + d, ny)
                    ys_copy(y, frm_y, h, b).wait_recv()
                    total += ys[frm_y, h, b].astype(jnp.float32)

                @pl.when(b < ctx)
                def _():
                    part[y, h, b] = total.astype(jnp.bfloat16)

                @pl.when(b == ctx)
                def _():
                    acc[h] = total

        @pl.when(b < ctx)
        def _():
            rs_copy(b, ctx).start()

    @pl.loop(0, nc)
    def _(b):
        @pl.when(b > ctx)
        def _():
            rs_copy(ctx, b).wait_recv()
            for h in range(hpd):
                acc[h] += rs[b, h].astype(jnp.float32)

    for h in range(hpd):
        main, edge, count = hot(h)
        unit = (acc[h].astype(jnp.bfloat16).astype(jnp.float32) / count).astype(jnp.bfloat16)
        spread = dot_tn(main, unit).astype(jnp.bfloat16)
        for to in range(nh):
            tg[to, h] = spread[to * T:(to + 1) * T]
        tgx[h] = dot_tn(edge, unit)[:EDGE].astype(jnp.bfloat16)

    for d in range(1, nh):
        tg_copy(lax.rem(j + d, nh), j).start()

    @pl.when((ctx < nc - 1))
    def _():
        @pl.when((ctx >= 0))
        def _():
            tx_copy(ctx + 1, j).start()

    own_tg = pltpu.make_async_copy(tg.at[j], rt.at[j], loc.at[0])
    own_tg.start()

    for d in range(1, nh):
        to = lax.rem(j + d, nh)
        tok_copy(to, j, 0).wait_send()
        tok_copy(to, j, 1).wait_send()

    @pl.when((j == 0) & (ctx > 0))
    def _():
        for to in range(nh):
            ext_copy(ctx - 1, to, 0).wait_send()
            ext_copy(ctx - 1, to, 1).wait_send()

    for d in range(1, ny):
        thr_copy(lax.rem(y + d, ny), y).wait_send()
    for yy in range(ny):
        swap_copy(yy, 0, c).wait_send()
        swap_copy(yy, 1, c).wait_send()
        att_copy(yy).wait_send()
        att_in(yy).wait_recv()
        pltpu.make_async_copy(att.at[yy, :, c], heads(out_ref, yy * 2 + c), loc.at[3 + yy]).wait()

    @pl.loop(0, nz)
    def _(zs):
        @pl.when(zs > z)
        def _():
            ag_copy(zs, z, 0).wait_send()
            ag_copy(zs, z, 1).wait_send()

        @pl.when(zs <= z)
        def _():
            for d in range(1, ny):
                vy_copy(lax.rem(y + d, ny), y, zs).wait_send()
            for d in range(1, nx):
                to = lax.rem(x + d, nx)

                @pl.when(x_sees(to, zs))
                def _():
                    kx_copy(to, x, zs).wait_send()
                    for yy in range(ny):
                        vx_copy(to, x, yy, zs).wait_send()

    @pl.loop(0, nc)
    def _(b):
        @pl.when(b <= ctx)
        def _():
            for d in range(1, ny):
                yy = lax.rem(y + d, ny)
                ky_copy(yy, y, b).wait_send()
                for h in range(hpd):
                    ys_copy(yy, y, h, b).wait_send()

        @pl.when(b < ctx)
        def _():
            rs_copy(b, ctx).wait_send()

    own_tg.wait()
    for d in range(1, nh):
        tg_copy(j, lax.rem(j + d, nh)).wait_recv()
    for owner in range(nh):
        for h in range(hpd):
            rows = rt[owner, h].astype(jnp.float32)
            kg_ref[owner * hpd + h] = rows[:, :D]
            vg_ref[owner * hpd + h] = rows[:, D:]

    @pl.when((j == 0) & (ctx > 0))
    def _():
        for owner in range(nh):
            tx_copy(ctx, owner).wait_recv()
            for h in range(hpd):
                rows = rx[owner, h].astype(jnp.float32)
                kg_ref[owner * hpd + h, :EDGE] += rows[:, :D]
                vg_ref[owner * hpd + h, :EDGE] += rows[:, D:]

    for d in range(1, nh):
        tg_copy(lax.rem(j + d, nh), j).wait_send()

    @pl.when((ctx < nc - 1))
    def _():
        tx_copy(ctx + 1, j).wait_send()


def per_device(nc, nh, token_keys, token_values, queries, out_grad, slot_ids):
    heads_all, T, D = token_keys.shape
    group = queries.shape[2]
    hpd, context = slot_ids.shape
    R = queries.shape[1] * group
    stride = T // queries.shape[1]
    TB = T * nh
    S = TB // RATIO
    ny = nh // 2
    nx = 2 ** ((nc.bit_length() - 1) // 2)
    nz = nc // nx
    ctx = lax.axis_index("ctx")
    padded = jnp.pad(slot_ids, ((0, 0), (0, LANES)), constant_values=context)
    window = lax.dynamic_slice_in_dim(padded, ctx * TB, TB + LANES, 1)
    relative = (window - ctx * S).reshape(hpd, 1, TB + LANES)
    seen_at = window[:, stride - 1:TB:stride]
    limit = jnp.repeat(seen_at.reshape(hpd, ny, 2, 1, R // group), group, axis=4)
    limit = limit.transpose(1, 0, 2, 3, 4)
    bf, f32 = jnp.bfloat16, jnp.float32
    dma = pltpu.SemaphoreType.DMA
    anywhere = pl.BlockSpec(memory_space=pl.ANY)
    vmem = pl.BlockSpec(memory_space=pltpu.VMEM)
    attended, key_grad, value_grad = pl.pallas_call(
        functools.partial(kernel, (nc, nx, nh, hpd, T, R, S, D)),
        out_shape=(
            jax.ShapeDtypeStruct((heads_all, R, D), bf),
            jax.ShapeDtypeStruct((heads_all, T, D), f32),
            jax.ShapeDtypeStruct((heads_all, T, D), f32),
        ),
        in_specs=[anywhere] * 4 + [vmem, vmem],
        out_specs=(anywhere, vmem, vmem),
        scratch_shapes=[
            pltpu.VMEM((ny, hpd, 2, R, D), bf),
            pltpu.VMEM((ny, hpd, 2, R, D), bf),
            pltpu.VMEM((hpd, nh, T, D), bf),
            pltpu.VMEM((hpd, nh, T, D), bf),
            pltpu.VMEM((hpd, LANES, D), bf),
            pltpu.VMEM((hpd, LANES, D), bf),
            pltpu.VMEM((ny, hpd, 2, 1, R), jnp.int32),
            pltpu.VMEM((ny, hpd, nc, S, D), bf),
            pltpu.VMEM((ny, hpd, nc, S, D), bf),
            pltpu.VMEM((ny, hpd, 2, R, D), bf),
            pltpu.VMEM((ny, hpd, nc, S, 2 * D), bf),
            pltpu.VMEM((ny, hpd, nc, S, 2 * D), bf),
            pltpu.VMEM((nc, hpd, S, 2 * D), bf),
            pltpu.VMEM((hpd, S, 2 * D), f32),
            pltpu.VMEM((nh, hpd, T, 2 * D), bf),
            pltpu.VMEM((hpd, EDGE, 2 * D), bf),
            pltpu.VMEM((nh, hpd, T, 2 * D), bf),
            pltpu.VMEM((nh, hpd, EDGE, 2 * D), bf),
            dma((ny,)), dma((ny,)), dma((ny,)), dma((ny,)), dma((3 + 2 * ny,)),
            dma((nh, 2)), dma((nh, 2)), dma((nh, 2)), dma((2,)), dma((ny,)), dma((ny,)),
            dma((nz, 2)), dma((nz, 2)), dma((nx, nz)), dma((nx, nz)), dma((ny, nc)), dma((ny, nc)),
            dma((ny, nz)), dma((ny, nz)), dma((nx, ny, nz)), dma((nx, ny, nz)), dma((ny,)), dma((ny,)),
            dma((ny, hpd, nc)), dma((ny, hpd, nc)), dma((nc,)), dma((nc,)),
            dma((nh,)), dma((nh,)), dma(()), dma((nh,)),
        ],
        compiler_params=pltpu.CompilerParams(
            collective_id=0, has_side_effects=True, vmem_limit_bytes=56 << 20
        ),
    )(
        queries.reshape(heads_all, R, D), out_grad.reshape(heads_all, R, D),
        token_keys, token_values, relative, limit,
    )
    return attended.reshape(queries.shape), key_grad, value_grad


def solution(mesh):
    nc, nh = mesh.shape["ctx"], mesh.shape["head"]
    rows = P(None, ("ctx", "head"), None)
    grouped = P(None, ("ctx", "head"), None, None)
    return jax.shard_map(
        functools.partial(per_device, nc, nh),
        mesh=mesh,
        in_specs=(rows, rows, grouped, grouped, P("head", None)),
        out_specs=(grouped, rows, rows),
        check_vma=False,
    )
```

```python
import functools
import math

import jax
import jax.numpy as jnp
from jax import lax
from jax.experimental import pallas as pl
from jax.experimental.pallas import tpu as pltpu
from jax.sharding import PartitionSpec as P

RATIO = 4
EDGE = 16
LANES = 128
MESH = pl.DeviceIdType.MESH
neg_big = -1e30


def dot_nt(a, b):
    return lax.dot_general(a, b, (((1,), (1,)), ((), ())), preferred_element_type=jnp.float32)


def dot_tn(a, b):
    return lax.dot_general(a, b, (((0,), (0,)), ((), ())), preferred_element_type=jnp.float32)


def dot_nn(a, b):
    return lax.dot_general(a, b, (((1,), (0,)), ((), ())), preferred_element_type=jnp.float32)


def kernel(
    dims,
    q_ref, g_ref, k_ref, v_ref, id_ref, thr_ref,
    out_ref, kg_ref, vg_ref,
    qb, gb, tk, tv, ek, ev, thrb, pk, pv, att, part, ys, rs, acc, tg, tgx, rt, rx,
    q_s, q_r, g_s, g_r, loc, tok_s, tok_r, ext_s, ext_r, thr_s, thr_r,
    ag_s, ag_r, kx_s, kx_r, ky_s, ky_r, vy_s, vy_r, vx_s, vx_r, at_s, at_r,
    ys_s, ys_r, rs_s, rs_r, tg_s, tg_r, tx_s, tx_r,
):
    nc, nx, nh, hpd, T, R, S, D = dims
    ny, nz = nh // 2, nc // nx
    TB = T * nh
    NS = nc * S
    scale = 1.0 / math.sqrt(D)
    ctx = lax.axis_index("ctx")
    j = lax.axis_index("head")
    y, c = j // 2, lax.rem(j, 2)
    peer = y * 2 + 1 - c
    z, x = ctx // nx, lax.rem(ctx, nx)

    def remote(src, dst, ssem, rsem, to_ctx, to_head):
        return pltpu.make_async_remote_copy(
            src_ref=src, dst_ref=dst, send_sem=ssem, recv_sem=rsem,
            device_id=(to_ctx, to_head), device_id_type=MESH,
        )

    def heads(ref, owner):
        return ref.at[pl.ds(owner * hpd, hpd)]

    ek[...] = jnp.zeros_like(ek)
    ev[...] = jnp.zeros_like(ev)
    rx[...] = jnp.zeros_like(rx)

    @pl.loop(0, nc)
    def _(b):
        @pl.when(b > ctx)
        def _():
            for yy in range(ny):
                for h in range(hpd):
                    pk[yy, h, b] = jnp.zeros((S, D), jnp.bfloat16)
                    pv[yy, h, b] = jnp.zeros((S, D), jnp.bfloat16)

    barrier = pltpu.get_barrier_semaphore()
    me = ctx * nh + j

    @pl.loop(1, nc * nh)
    def _(i):
        other = lax.rem(me + i, nc * nh)
        pl.semaphore_signal(
            barrier, inc=1, device_id=(other // nh, lax.rem(other, nh)), device_id_type=MESH
        )

    pl.semaphore_wait(barrier, nc * nh - 1)

    def tok_copy(to, frm, kv):
        src, dst = ((k_ref, tk), (v_ref, tv))[kv]
        return remote(heads(src, to), dst.at[:, frm], tok_s.at[to, kv], tok_r.at[frm, kv], ctx, to)

    def ext_copy(to_ctx, to, kv):
        src, dst = ((k_ref, ek), (v_ref, ev))[kv]
        return remote(
            src.at[pl.ds(to * hpd, hpd), pl.ds(0, EDGE)], dst.at[:, pl.ds(0, EDGE)],
            ext_s.at[to, kv], ext_r.at[kv], to_ctx, to,
        )

    def thr_copy(to_y, frm_y):
        return remote(thr_ref.at[:, to_y], thrb.at[frm_y], thr_s.at[to_y], thr_r.at[frm_y], ctx, to_y * 2 + c)

    def swap_copy(yy, kv, core):
        src, dst, ss, sr = ((q_ref, qb, q_s, q_r), (g_ref, gb, g_s, g_r))[kv]
        return remote(
            heads(src, yy * 2 + 1 - c), dst.at[yy, :, core], ss.at[yy], sr.at[yy], ctx, peer
        )

    def ag_copy(to_z, frm_z, kv):
        blk = (pk, pv)[kv].at[y, :, frm_z * nx + x]
        return remote(blk, blk, ag_s.at[to_z, kv], ag_r.at[frm_z, kv], to_z * nx + x, j)

    def kx_copy(to_x, frm_x, zs):
        blk = pk.at[y, :, zs * nx + frm_x]
        return remote(blk, blk, kx_s.at[to_x, zs], kx_r.at[frm_x, zs], z * nx + to_x, j)

    def ky_copy(to_y, frm_y, b):
        blk = pk.at[frm_y, :, b]
        return remote(blk, blk, ky_s.at[to_y, b], ky_r.at[frm_y, b], ctx, to_y * 2 + c)

    def vy_copy(to_y, frm_y, zs):
        blk = pv.at[frm_y, :, zs * nx + x]
        return remote(blk, blk, vy_s.at[to_y, zs], vy_r.at[frm_y, zs], ctx, to_y * 2 + c)

    def vx_copy(to_x, frm_x, yy, zs):
        blk = pv.at[yy, :, zs * nx + frm_x]
        return remote(blk, blk, vx_s.at[to_x, yy, zs], vx_r.at[frm_x, yy, zs], z * nx + to_x, j)

    def x_sees(to_x, zs):
        return (zs < z) | ((zs == z) & (to_x > x))

    def x_gives(frm_x, zs):
        return (zs < z) | ((zs == z) & (frm_x < x))

    def att_copy(yy):
        return remote(att.at[yy, :, 1 - c], heads(out_ref, yy * 2 + c), at_s.at[yy], at_r.at[yy], ctx, peer)

    def att_in(yy):
        return remote(att.at[yy, :, 1 - c], heads(out_ref, yy * 2 + 1 - c), at_s.at[yy], at_r.at[yy], ctx, peer)

    def ys_copy(to_y, frm_y, h, b):
        return remote(
            part.at[to_y, h, b], ys.at[frm_y, h, b], ys_s.at[to_y, h, b], ys_r.at[frm_y, h, b], ctx, to_y * 2 + c
        )

    def rs_copy(b, frm_ctx):
        return remote(part.at[y, :, b], rs.at[frm_ctx], rs_s.at[b], rs_r.at[frm_ctx], b, j)

    def tg_copy(to, frm):
        return remote(tg.at[to], rt.at[frm], tg_s.at[to], tg_r.at[frm], ctx, to)

    def tx_copy(to_ctx, frm):
        return remote(tgx, rx.at[frm], tx_s, tx_r.at[frm], to_ctx, 0)

    for d in range(1, nh):
        to = lax.rem(j + d, nh)
        tok_copy(to, j, 0).start()
        tok_copy(to, j, 1).start()

    @pl.when((j == 0) & (ctx > 0))
    def _():
        for to in range(nh):
            ext_copy(ctx - 1, to, 0).start()
            ext_copy(ctx - 1, to, 1).start()

    own_tok = [
        pltpu.make_async_copy(heads(k_ref, j), tk.at[:, j], loc.at[0]),
        pltpu.make_async_copy(heads(v_ref, j), tv.at[:, j], loc.at[1]),
    ]
    own_thr = pltpu.make_async_copy(thr_ref.at[:, y], thrb.at[y], loc.at[2])
    for cp in own_tok:
        cp.start()
    own_thr.start()
    for d in range(1, ny):
        thr_copy(lax.rem(y + d, ny), y).start()
    own_rows = []
    for d in range(ny):
        yy = lax.rem(y + d, ny)
        swap_copy(yy, 0, c).start()
        swap_copy(yy, 1, c).start()
        own_rows.append(
            pltpu.make_async_copy(heads(q_ref, yy * 2 + c), qb.at[yy, :, c], loc.at[3 + 2 * d])
        )
        own_rows.append(
            pltpu.make_async_copy(heads(g_ref, yy * 2 + c), gb.at[yy, :, c], loc.at[4 + 2 * d])
        )
    for cp in own_rows:
        cp.start()

    for d in range(1, nh):
        frm = lax.rem(j + d, nh)
        tok_copy(j, frm, 0).wait_recv()
        tok_copy(j, frm, 1).wait_recv()

    @pl.when(ctx < nc - 1)
    def _():
        ext_copy(ctx, j, 0).wait_recv()
        ext_copy(ctx, j, 1).wait_recv()

    for cp in own_tok:
        cp.wait()

    def hot(h):
        rel = id_ref[h:h + 1]
        main = lax.broadcasted_iota(jnp.int32, (S, TB), 0) == rel[:, :TB]
        edge = lax.broadcasted_iota(jnp.int32, (S, LANES), 0) == rel[:, TB:]
        main, edge = main.astype(jnp.float32), edge.astype(jnp.float32)
        count = jnp.sum(main, axis=1, keepdims=True) + jnp.sum(edge, axis=1, keepdims=True)
        return main.astype(jnp.bfloat16), edge.astype(jnp.bfloat16), count

    for h in range(hpd):
        main, edge, count = hot(h)
        keys = dot_nn(main, tk[h].reshape(TB, D)) + dot_nn(edge, ek[h])
        vals = dot_nn(main, tv[h].reshape(TB, D)) + dot_nn(edge, ev[h])
        pk[y, h, ctx] = (keys / count).astype(jnp.bfloat16)
        pv[y, h, ctx] = (vals / count).astype(jnp.bfloat16)

    def spread_block(zs):
        for d in range(1, nx):
            to = lax.rem(x + d, nx)

            @pl.when(x_sees(to, zs))
            def _():
                kx_copy(to, x, zs).start()

        for d in range(1, ny):
            to = lax.rem(y + d, ny)
            vy_copy(to, y, zs).start()
            ky_copy(to, y, zs * nx + x).start()

        for d in range(1, nx):
            to = lax.rem(x + d, nx)

            @pl.when(x_sees(to, zs))
            def _():
                vx_copy(to, x, y, zs).start()

    @pl.loop(0, nz)
    def _(i):
        to = nz - 1 - i

        @pl.when(to > z)
        def _():
            ag_copy(to, z, 0).start()
            ag_copy(to, z, 1).start()

    spread_block(z)

    for cp in own_rows:
        cp.wait()
    own_thr.wait()
    for d in range(ny):
        yy = lax.rem(y + d, ny)
        swap_copy(yy, 0, 1 - c).wait_recv()
        swap_copy(yy, 1, 1 - c).wait_recv()

    @pl.loop(0, nz)
    def _(i):
        zs = nz - 1 - i

        @pl.when(zs < z)
        def _():
            ag_copy(z, zs, 0).wait_recv()
            ag_copy(z, zs, 1).wait_recv()
            spread_block(zs)

    @pl.loop(0, nz)
    def _(i):
        zs = nz - 1 - i

        @pl.when(zs <= z)
        def _():
            for d in range(1, nx):
                frm = lax.rem(x + d, nx)

                @pl.when(x_gives(frm, zs))
                def _():
                    kx_copy(x, frm, zs).wait_recv()
                    for e in range(1, ny):
                        ky_copy(lax.rem(y + e, ny), y, zs * nx + frm).start()

            for e in range(1, ny):
                frm_y = lax.rem(y + e, ny)
                vy_copy(y, frm_y, zs).wait_recv()
                for d in range(1, nx):
                    to = lax.rem(x + d, nx)

                    @pl.when(x_sees(to, zs))
                    def _():
                        vx_copy(to, x, frm_y, zs).start()

    def wait_vals(yy):
        @pl.loop(0, nz)
        def _(zs):
            for d in range(1, nx):
                frm = lax.rem(x + d, nx)

                @pl.when(x_gives(frm, zs))
                def _():
                    vx_copy(x, frm, yy, zs).wait_recv()

    @pl.loop(0, ny)
    def _(k):
        yy = lax.rem(y + k, ny)

        @pl.when(k > 0)
        def _():
            thr_copy(y, yy).wait_recv()

            @pl.loop(0, nc)
            def _(b):
                @pl.when(b <= ctx)
                def _():
                    ky_copy(y, yy, b).wait_recv()

        wait_vals(yy)

        @pl.loop(0, hpd)
        def _(h):
            keys, vals = pk[yy, h].reshape(NS, D), pv[yy, h].reshape(NS, D)
            slot = lax.broadcasted_iota(jnp.int32, (NS, R), 0)
            key_sum = val_sum = None
            for core in range(2):
                rows, grads = qb[yy, h, core], gb[yy, h, core]
                scores = jnp.where(slot <= thrb[yy, h, core], dot_nt(keys, rows), neg_big)
                top = jnp.max(scores, axis=0, keepdims=True)
                raw = jnp.exp2((scores - top) * (scale * math.log2(math.e)))
                weights = raw * (1.0 / jnp.sum(raw, axis=0, keepdims=True))
                low = weights.astype(jnp.bfloat16)
                seen = dot_tn(vals, low).astype(jnp.bfloat16).astype(jnp.float32)
                grads_t = grads.astype(jnp.float32).T
                row_dot = jnp.sum(grads_t * seen, axis=0, keepdims=True)
                att[yy, h, core] = seen.T.astype(jnp.bfloat16)
                slope = (weights * (dot_nt(vals, grads) - row_dot)).astype(jnp.bfloat16)
                val_grad = dot_nn(low, grads)
                key_grad = dot_nn(slope, rows)
                key_sum = key_grad if key_sum is None else key_sum + key_grad
                val_sum = val_grad if val_sum is None else val_sum + val_grad
            part[yy, h, :, :, :D] = (key_sum * scale).astype(jnp.bfloat16).reshape(nc, S, D)
            part[yy, h, :, :, D:] = val_sum.astype(jnp.bfloat16).reshape(nc, S, D)

            @pl.when(k > 0)
            def _():
                @pl.loop(0, nc)
                def _(b):
                    @pl.when(b <= ctx)
                    def _():
                        ys_copy(yy, y, h, b).start()

        att_copy(yy).start()
        pltpu.make_async_copy(att.at[yy, :, c], heads(out_ref, yy * 2 + c), loc.at[3 + yy]).start()

    @pl.loop(0, nc)
    def _(b):
        @pl.when(b <= ctx)
        def _():
            for h in range(hpd):
                total = part[y, h, b].astype(jnp.float32)
                for d in range(1, ny):
                    frm_y = lax.rem(y + d, ny)
                    ys_copy(y, frm_y, h, b).wait_recv()
                    total += ys[frm_y, h, b].astype(jnp.float32)

                @pl.when(b < ctx)
                def _():
                    part[y, h, b] = total.astype(jnp.bfloat16)

                @pl.when(b == ctx)
                def _():
                    acc[h] = total

        @pl.when(b < ctx)
        def _():
            rs_copy(b, ctx).start()

    @pl.loop(0, nc)
    def _(b):
        @pl.when(b > ctx)
        def _():
            rs_copy(ctx, b).wait_recv()
            for h in range(hpd):
                acc[h] += rs[b, h].astype(jnp.float32)

    for h in range(hpd):
        main, edge, count = hot(h)
        unit = (acc[h].astype(jnp.bfloat16).astype(jnp.float32) / count).astype(jnp.bfloat16)
        spread = dot_tn(main, unit).astype(jnp.bfloat16)
        for to in range(nh):
            tg[to, h] = spread[to * T:(to + 1) * T]
        tgx[h] = dot_tn(edge, unit)[:EDGE].astype(jnp.bfloat16)

    for d in range(1, nh):
        tg_copy(lax.rem(j + d, nh), j).start()

    @pl.when((ctx < nc - 1))
    def _():
        @pl.when((ctx >= 0))
        def _():
            tx_copy(ctx + 1, j).start()

    own_tg = pltpu.make_async_copy(tg.at[j], rt.at[j], loc.at[0])
    own_tg.start()

    for d in range(1, nh):
        to = lax.rem(j + d, nh)
        tok_copy(to, j, 0).wait_send()
        tok_copy(to, j, 1).wait_send()

    @pl.when((j == 0) & (ctx > 0))
    def _():
        for to in range(nh):
            ext_copy(ctx - 1, to, 0).wait_send()
            ext_copy(ctx - 1, to, 1).wait_send()

    for d in range(1, ny):
        thr_copy(lax.rem(y + d, ny), y).wait_send()
    for yy in range(ny):
        swap_copy(yy, 0, c).wait_send()
        swap_copy(yy, 1, c).wait_send()
        att_copy(yy).wait_send()
        att_in(yy).wait_recv()
        pltpu.make_async_copy(att.at[yy, :, c], heads(out_ref, yy * 2 + c), loc.at[3 + yy]).wait()

    @pl.loop(0, nz)
    def _(zs):
        @pl.when(zs > z)
        def _():
            ag_copy(zs, z, 0).wait_send()
            ag_copy(zs, z, 1).wait_send()

        @pl.when(zs <= z)
        def _():
            for d in range(1, ny):
                vy_copy(lax.rem(y + d, ny), y, zs).wait_send()
            for d in range(1, nx):
                to = lax.rem(x + d, nx)

                @pl.when(x_sees(to, zs))
                def _():
                    kx_copy(to, x, zs).wait_send()
                    for yy in range(ny):
                        vx_copy(to, x, yy, zs).wait_send()

    @pl.loop(0, nc)
    def _(b):
        @pl.when(b <= ctx)
        def _():
            for d in range(1, ny):
                yy = lax.rem(y + d, ny)
                ky_copy(yy, y, b).wait_send()
                for h in range(hpd):
                    ys_copy(yy, y, h, b).wait_send()

        @pl.when(b < ctx)
        def _():
            rs_copy(b, ctx).wait_send()

    own_tg.wait()
    for d in range(1, nh):
        tg_copy(j, lax.rem(j + d, nh)).wait_recv()
    for owner in range(nh):
        for h in range(hpd):
            rows = rt[owner, h].astype(jnp.float32)
            kg_ref[owner * hpd + h] = rows[:, :D]
            vg_ref[owner * hpd + h] = rows[:, D:]

    @pl.when((j == 0) & (ctx > 0))
    def _():
        for owner in range(nh):
            tx_copy(ctx, owner).wait_recv()
            for h in range(hpd):
                rows = rx[owner, h].astype(jnp.float32)
                kg_ref[owner * hpd + h, :EDGE] += rows[:, :D]
                vg_ref[owner * hpd + h, :EDGE] += rows[:, D:]

    for d in range(1, nh):
        tg_copy(lax.rem(j + d, nh), j).wait_send()

    @pl.when((ctx < nc - 1))
    def _():
        tx_copy(ctx + 1, j).wait_send()


def hand_over(a_ref, k_ref, v_ref, a_out, k_out, v_out):
    a_out[...] = a_ref[...]
    k_out[...] = k_ref[...]
    v_out[...] = v_ref[...]


def per_device(nc, nh, token_keys, token_values, queries, out_grad, slot_ids):
    heads_all, T, D = token_keys.shape
    group = queries.shape[2]
    hpd, context = slot_ids.shape
    R = queries.shape[1] * group
    stride = T // queries.shape[1]
    TB = T * nh
    S = TB // RATIO
    ny = nh // 2
    nx = 2 ** ((nc.bit_length() - 1) // 2)
    nz = nc // nx
    ctx = lax.axis_index("ctx")
    padded = jnp.pad(slot_ids, ((0, 0), (0, LANES)), constant_values=context)
    window = lax.dynamic_slice_in_dim(padded, ctx * TB, TB + LANES, 1)
    relative = window - ctx * S
    seen_at = window[:, stride - 1:TB:stride]
    limit = jnp.repeat(seen_at.reshape(hpd, ny, 2, 1, R // group), group, axis=4)
    bf, f32 = jnp.bfloat16, jnp.float32
    dma = pltpu.SemaphoreType.DMA
    anywhere = pl.BlockSpec(memory_space=pl.ANY)
    vmem = pl.BlockSpec(memory_space=pltpu.VMEM)
    attended, key_grad, value_grad = pl.pallas_call(
        functools.partial(kernel, (nc, nx, nh, hpd, T, R, S, D)),
        out_shape=(
            jax.ShapeDtypeStruct((heads_all, R, D), bf),
            jax.ShapeDtypeStruct((heads_all, T, D), f32),
            jax.ShapeDtypeStruct((heads_all, T, D), f32),
        ),
        in_specs=[anywhere] * 4 + [vmem, vmem],
        out_specs=(anywhere, vmem, vmem),
        scratch_shapes=[
            pltpu.VMEM((ny, hpd, 2, R, D), bf),
            pltpu.VMEM((ny, hpd, 2, R, D), bf),
            pltpu.VMEM((hpd, nh, T, D), bf),
            pltpu.VMEM((hpd, nh, T, D), bf),
            pltpu.VMEM((hpd, LANES, D), bf),
            pltpu.VMEM((hpd, LANES, D), bf),
            pltpu.VMEM((ny, hpd, 2, 1, R), jnp.int32),
            pltpu.VMEM((ny, hpd, nc, S, D), bf),
            pltpu.VMEM((ny, hpd, nc, S, D), bf),
            pltpu.VMEM((ny, hpd, 2, R, D), bf),
            pltpu.VMEM((ny, hpd, nc, S, 2 * D), bf),
            pltpu.VMEM((ny, hpd, nc, S, 2 * D), bf),
            pltpu.VMEM((nc, hpd, S, 2 * D), bf),
            pltpu.VMEM((hpd, S, 2 * D), f32),
            pltpu.VMEM((nh, hpd, T, 2 * D), bf),
            pltpu.VMEM((hpd, EDGE, 2 * D), bf),
            pltpu.VMEM((nh, hpd, T, 2 * D), bf),
            pltpu.VMEM((nh, hpd, EDGE, 2 * D), bf),
            dma((ny,)), dma((ny,)), dma((ny,)), dma((ny,)), dma((3 + 2 * ny,)),
            dma((nh, 2)), dma((nh, 2)), dma((nh, 2)), dma((2,)), dma((ny,)), dma((ny,)),
            dma((nz, 2)), dma((nz, 2)), dma((nx, nz)), dma((nx, nz)), dma((ny, nc)), dma((ny, nc)),
            dma((ny, nz)), dma((ny, nz)), dma((nx, ny, nz)), dma((nx, ny, nz)), dma((ny,)), dma((ny,)),
            dma((ny, hpd, nc)), dma((ny, hpd, nc)), dma((nc,)), dma((nc,)),
            dma((nh,)), dma((nh,)), dma(()), dma((nh,)),
        ],
        compiler_params=pltpu.CompilerParams(
            collective_id=0, has_side_effects=True, vmem_limit_bytes=56 << 20
        ),
    )(
        queries.reshape(heads_all, R, D), out_grad.reshape(heads_all, R, D),
        token_keys, token_values, relative, limit,
    )
    results = (attended, key_grad, value_grad)

    def by_head(r):
        return pl.BlockSpec((heads_all // 2,) + r.shape[1:], lambda i: (i, 0, 0))

    attended, key_grad, value_grad = pl.pallas_call(
        hand_over,
        out_shape=tuple(jax.ShapeDtypeStruct(r.shape, r.dtype) for r in results),
        grid=(2,),
        in_specs=[by_head(r) for r in results],
        out_specs=tuple(by_head(r) for r in results),
    )(*results)
    return attended.reshape(queries.shape), key_grad, value_grad


def solution(mesh):
    nc, nh = mesh.shape["ctx"], mesh.shape["head"]
    rows = P(None, ("ctx", "head"), None)
    grouped = P(None, ("ctx", "head"), None, None)
    return jax.shard_map(
        functools.partial(per_device, nc, nh),
        mesh=mesh,
        in_specs=(rows, rows, grouped, grouped, P("head", None)),
        out_specs=(grouped, rows, rows),
        check_vma=False,
    )
```
